256 devices in a mesh: seq: 64 (over y, z, core), head: 4 (over x).
Axes of the slice: x: 4, y: 4, z: 8, core: 2. Of those that a mesh axis runs over, the one named last changes fastest.
Arguments:
- queries: bfloat16 [32768, 8192], P('seq', 'head'), may hold values from -6 to 6
- keys: bfloat16 [32768, 8192], P('seq', 'head'), may hold values from -0.52734375 to 0.52734375
- values: bfloat16 [32768, 8192], P('seq', 'head'), may hold values from -6 to 6
- suffix_keys: bfloat16 [256, 128, 8192], P('seq', None, 'head'), may hold values from -0.52734375 to 0.52734375
- suffix_values: bfloat16 [256, 128, 8192], P('seq', None, 'head'), may hold values from -6 to 6
- suffix_lengths: int32 [256], P('seq'), may hold values from 1 to 128
- step_queries: bfloat16 [2, 256, 8192], P(None, 'seq', 'head'), may hold values from -6 to 6
- step_keys: bfloat16 [2, 256, 8192], P(None, 'seq', 'head'), may hold values from -0.52734375 to 0.52734375
- step_values: bfloat16 [2, 256, 8192], P(None, 'seq', 'head'), may hold values from -6 to 6
- norm_gain: float32 [8192], P('head'), may hold values from 0.1 to 1.9
Outputs:
- prompt_out: bfloat16 [32768, 8192], P('seq', 'head')
- decoded: bfloat16 [2, 256, 8192], P(None, 'seq', 'head')
The draws below stay inside these ranges and needn't reach their ends.
All inputs are finite; a program needn't handle non-finite values.
Results may differ from the reference program's by a relative error of at most 0.005.
Values sent between devices are 32-bit elements; how exact they have to be, the bound alone decides.
A program may use at most 128 MiB of HBM per device.

```python
import jax
import jax.numpy as jnp
from jax import lax

HEADS = 64
HEAD_DIM = 128
SPAN = 512
SUF = 128
STEPS = 2
WIDTH = 8192
PROMPT = 32768
SAMPLES = 256
N_SEQ = 64


def plant(result, rng, least, largest):
    spot = [jax.random.randint(jax.random.fold_in(rng, axis), (), 0, length) for axis, length in enumerate(result.shape)]
    main_axis = result.shape.index(max(result.shape))
    next_to = spot[:main_axis] + [(spot[main_axis] + 1) % result.shape[main_axis]] + spot[main_axis + 1:]
    return result.at[tuple(spot)].set(least).at[tuple(next_to)].set(largest)


def levels(key, extent, cuts, low, high):
    factor_of, own = 1.0, jax.random.fold_in(key, 6)
    for axis_at, shards_of in cuts:
        steps = jnp.exp(jax.random.uniform(jax.random.fold_in(own, axis_at), (shards_of,), jnp.float32, low / len(cuts), high / len(cuts)))
        factor_of = factor_of * jnp.repeat(steps, extent[axis_at] // shards_of).reshape([-1 if axis == axis_at else 1 for axis in range(len(extent))])
    return factor_of


def noise(rng, shape, width, limit, shards=(), held_as=jnp.bfloat16):
    loudness = levels(rng, shape, shards, -0.22, 0.18) if shards else 1.0
    values = jax.random.normal(rng, shape, jnp.float32) * width * loudness
    return jnp.minimum(jnp.maximum(values, -limit), limit).astype(held_as)


def setup_inputs(seed: int = 0) -> dict:
    arg_keys = jax.random.split(jax.random.key(seed), 11)
    queries = noise(arg_keys[0], (PROMPT, WIDTH), 1.0, 6.0, ((0, 64), (1, 4)))
    keys = noise(arg_keys[1], (PROMPT, WIDTH), 0.088, 0.52734375, ((0, 64), (1, 4)))
    values = noise(arg_keys[2], (PROMPT, WIDTH), 1.0, 6.0, ((0, 64), (1, 4)))
    suffix_keys = noise(arg_keys[3], (SAMPLES, SUF, WIDTH), 0.088, 0.52734375, ((0, 64), (2, 4)))
    suffix_values = noise(arg_keys[4], (SAMPLES, SUF, WIDTH), 1.0, 6.0, ((0, 64), (2, 4)))
    suffix_lengths = plant(jax.random.randint(arg_keys[5], (SAMPLES,), 1, SUF + 1), jax.random.fold_in(arg_keys[5], 1), 1, SUF).astype(jnp.int32)
    step_queries = noise(arg_keys[6], (STEPS, SAMPLES, WIDTH), 1.0, 6.0, ((1, 64), (2, 4)))
    step_keys = noise(arg_keys[7], (STEPS, SAMPLES, WIDTH), 0.088, 0.52734375, ((1, 64), (2, 4)))
    step_values = noise(arg_keys[8], (STEPS, SAMPLES, WIDTH), 1.0, 6.0, ((1, 64), (2, 4)))
    norm_gain = jnp.clip(1.0 + 0.18 * jax.random.normal(arg_keys[9], (WIDTH,), jnp.float32), 0.1, 1.9)
    return {"queries": queries, "keys": keys, "values": values, "suffix_keys": suffix_keys, "suffix_values": suffix_values, "suffix_lengths": suffix_lengths, "step_queries": step_queries, "step_keys": step_keys, "step_values": step_values, "norm_gain": norm_gain}


HIGHEST_PREC = lax.Precision.HIGHEST

def normalize(raw, norm_gain):
    mean_sq = lax.optimization_barrier(jnp.mean(raw * raw, axis=-1, keepdims=True))
    return (raw * lax.rsqrt(mean_sq + 1e-06) * norm_gain).astype(jnp.bfloat16)

def reference(queries, keys, values, suffix_keys, suffix_values, suffix_lengths, step_queries, step_keys, step_values, norm_gain):
    all_queries = queries.reshape(N_SEQ, SPAN, HEADS, HEAD_DIM).astype(jnp.float32)
    all_keys = keys.reshape(N_SEQ, SPAN, HEADS, HEAD_DIM).astype(jnp.float32)
    all_values = values.reshape(N_SEQ, SPAN, HEADS, HEAD_DIM).astype(jnp.float32)
    positions = jnp.arange(SPAN, dtype=jnp.int32)
    causal = positions[None, :] <= positions[:, None]

    def block_step(state, inputs):
        block_queries, block_keys, block_values = inputs
        scores = jnp.einsum('chd,shd->hcs', block_queries, block_keys, precision=HIGHEST_PREC)
        scores = jnp.where(causal[None], scores, 0.0).astype(jnp.bfloat16)
        scores = lax.optimization_barrier(scores).astype(jnp.float32)
        intra = jnp.einsum('hcs,she->che', scores, block_values, precision=HIGHEST_PREC)
        prior_low = lax.optimization_barrier(state.astype(jnp.bfloat16)).astype(jnp.float32)
        inter = jnp.einsum('chd,hde->che', block_queries, prior_low, precision=HIGHEST_PREC)
        attended = intra + inter
        new_state = state + jnp.einsum('chd,che->hde', block_keys, block_values, precision=HIGHEST_PREC)
        return (new_state, attended)
    zero = jnp.zeros((HEADS, HEAD_DIM, HEAD_DIM), jnp.float32)
    final, attended = lax.scan(block_step, zero, (all_queries, all_keys, all_values))
    prompt_out = normalize(attended.reshape(PROMPT, WIDTH), norm_gain)
    live = (jnp.arange(SUF, dtype=jnp.int32)[None, :] < suffix_lengths[:, None]).astype(jnp.float32)
    masked_keys = suffix_keys.reshape(SAMPLES, SUF, HEADS, HEAD_DIM).astype(jnp.float32) * live[:, :, None, None]
    suffix_vals = suffix_values.reshape(SAMPLES, SUF, HEADS, HEAD_DIM).astype(jnp.float32)
    state = final[None] + jnp.einsum('bjhd,bjhe->bhde', masked_keys, suffix_vals, precision=HIGHEST_PREC)
    outputs = []
    for step in range(STEPS):
        new_keys = step_keys[step].reshape(SAMPLES, HEADS, HEAD_DIM).astype(jnp.float32)
        new_vals = step_values[step].reshape(SAMPLES, HEADS, HEAD_DIM).astype(jnp.float32)
        new_query = step_queries[step].reshape(SAMPLES, HEADS, HEAD_DIM).astype(jnp.float32)
        state = state + jnp.einsum('bhd,bhe->bhde', new_keys, new_vals, precision=HIGHEST_PREC)
        raw = jnp.einsum('bhd,bhde->bhe', new_query, state, precision=HIGHEST_PREC)
        outputs.append(raw.reshape(SAMPLES, WIDTH))
    decoded = normalize(jnp.stack(outputs), norm_gain)
    return (prompt_out, decoded)
```

```python
import jax
import jax.numpy as jnp
from jax import lax
from jax.experimental import pallas as pl
from jax.experimental.pallas import tpu as pltpu
from jax.sharding import Mesh
from jax.sharding import PartitionSpec as P

D = 128
NY, NZ, NX = 4, 8, 4
AXES = {"sy": NY, "sz": NZ, "sc": 2, "head": NX}
SEQ = ("sy", "sz", "sc")
MESH = pl.DeviceIdType.MESH
F32 = jnp.float32
BF16 = jnp.bfloat16
FAR_FIRST = (4, 3, 5, 2, 6, 1, 7)
NEAR_FIRST = (1, 7, 2, 6, 3, 5, 4)


def dot(a, b, ca, cb):
    return lax.dot_general(a, b, (((ca,), (cb,)), ((), ())), preferred_element_type=F32)


def away(axis, step):
    size = AXES[axis]
    return {axis: lax.rem(lax.axis_index(axis) + step, size)}


def lanes(head):
    return pl.ds(pl.multiple_of(head * D, D), D)


def main_kernel(
    len_ref, q_hbm, k_hbm, v_hbm, sk_hbm, sv_hbm, tq_hbm, tk_hbm, tv_hbm,
    att_out, sums_out, raw_out,
    q, k, v, sk, sv, tq, tk, tv, q8, k8, v8, k8s, v8s, mask,
    att, attb, acc, own, xsend, xrecv, chip, recv1, rsend, yrecv, send3, recv3,
    fwd, frecv, msg, mrecv,
    ld, out_sem, x_s, x_r, a_s, a_r, y_s, y_r, b_s, b_r, f_s, f_r, g_s, g_r,
):
    y, z, c, x = (lax.axis_index(a) for a in ("sy", "sz", "sc", "head"))
    other = 1 - c
    partner = {"sc": other}
    barrier = pltpu.get_barrier_semaphore()
    peers = [partner]
    peers += [away("sz", d) for d in range(1, NZ)]
    peers += [away("sy", d) for d in range(1, NY)]
    peers += [away("head", d) for d in range(1, NX)]
    for peer in peers:
        pl.semaphore_signal(barrier, inc=1, device_id=peer, device_id_type=MESH)

    half = NZ * D
    theirs = pl.ds(pl.multiple_of(other * half, half), half)
    mine = pl.ds(pl.multiple_of(c * half, half), half)
    loads = []
    for src, dst in (
        (k_hbm.at[:, theirs], k.at[:, theirs]),
        (v_hbm.at[:, theirs], v.at[:, theirs]),
        (tq_hbm, tq),
        (k_hbm.at[:, mine], k.at[:, mine]),
        (v_hbm.at[:, mine], v.at[:, mine]),
        (q_hbm, q),
        (tk_hbm, tk),
        (tv_hbm, tv),
        (sk_hbm, sk),
        (sv_hbm, sv),
    ):
        copy = pltpu.make_async_copy(src, dst, ld.at[len(loads)])
        copy.start()
        loads.append(copy)

    def send(src, dst, s, r, peer):
        copy = pltpu.make_async_remote_copy(
            src_ref=src, dst_ref=dst, send_sem=s, recv_sem=r, device_id=peer, device_id_type=MESH
        )
        return copy

    loads[0].wait()
    loads[1].wait()
    loads[2].wait()
    q8[0:4, :] = tq[0].astype(F32)
    q8[4:8, :] = tq[1].astype(F32)

    def their_state(i, carry):
        cols = lanes(other * NZ + i)
        xsend[i, 0:D, :] = dot(k[:, cols], v[:, cols], 0, 0)
        xsend[i, D : D + 8, :] = q8[:, cols]
        return carry

    lax.fori_loop(0, NZ, their_state, 0)
    pl.semaphore_wait(barrier, len(peers))
    x_copies = []
    for i in range(NZ):
        copy = send(xsend.at[i], xrecv.at[i], x_s.at[i], x_r.at[i], partner)
        copy.start()
        x_copies.append(copy)

    loads[3].wait()
    loads[4].wait()

    def my_state(i, carry):
        cols = lanes(c * NZ + i)
        own[i] = dot(k[:, cols], v[:, cols], 0, 0)
        return carry

    lax.fori_loop(0, NZ, my_state, 0)
    for copy in x_copies:
        copy.wait_recv()

    def chip_sum(i, dst):
        dst[0:D, :] = own[i] + xrecv[i, 0:D, :]
        dst[D : D + 8, :] = q8[:, lanes(c * NZ + i)]
        dst[D + 8 : D + 16, :] = xrecv[i, D : D + 8, :]

    a_copies = {}
    for d in FAR_FIRST:
        i = lax.rem(z + d, NZ)
        chip_sum(i, chip.at[i])
        a_copies[d] = send(chip.at[i], recv1.at[z], a_s.at[d], a_r.at[d], away("sz", d))
        a_copies[d].start()
    chip_sum(z, recv1.at[z])

    loads[5].wait()
    rows = lax.broadcasted_iota(jnp.int32, (256, 256), 0)
    columns = lax.broadcasted_iota(jnp.int32, (256, 256), 1)
    causal = columns <= rows

    def intra(h, carry):
        cols = lanes(h)
        top, bottom = q[0:256, cols], q[256:512, cols]
        s00 = jnp.where(causal, dot(top, k[0:256, cols], 1, 1), 0.0).astype(BF16)
        att[0:256, cols] = dot(s00, v[0:256, cols], 1, 0)
        s10 = dot(bottom, k[0:256, cols], 1, 1).astype(BF16)
        s11 = jnp.where(causal, dot(bottom, k[256:512, cols], 1, 1), 0.0).astype(BF16)
        att[256:512, cols] = dot(s10, v[0:256, cols], 1, 0) + dot(s11, v[256:512, cols], 1, 0)
        return carry

    lax.fori_loop(0, 10, intra, 0)

    for d in FAR_FIRST:
        a_copies[d].wait_recv()
    total = recv1[0, 0:D, :]
    for j in range(1, NZ):
        total = total + recv1[j, 0:D, :]
    rsend[...] = total
    yrecv[y] = total
    y_copies = []
    for d in (2, 1, 3):
        copy = send(rsend, yrecv.at[y], y_s.at[d], y_r.at[d], away("sy", d))
        copy.start()
        y_copies.append(copy)

    for copy in loads[6:]:
        copy.wait()
    k8[0:4, :] = tk[0].astype(F32)
    k8[4:8, :] = tk[1].astype(F32)
    v8[0:4, :] = tv[0].astype(F32)
    v8[4:8, :] = tv[1].astype(F32)
    k8s[...] = jnp.zeros_like(k8s)
    v8s[...] = jnp.zeros_like(v8s)
    k8s[4:8, :] = tk[0].astype(F32)
    v8s[4:8, :] = tv[0].astype(F32)
    row = lax.rem(lax.broadcasted_iota(jnp.int32, (8, D), 0), 4)
    column = lax.broadcasted_iota(jnp.int32, (8, D), 1)
    for n in range(4):
        live = (row == n) & (column < len_ref[n])
        mask[:, n * D : (n + 1) * D] = jnp.where(live, 1.0, 0.0)

    def suffix(h, carry):
        cols = lanes(h)
        query = q8[:, cols]
        scores = dot(query.astype(BF16), sk[:, cols], 1, 1) * mask[...]
        high = scores.astype(BF16).astype(F32)
        both = jnp.concatenate([high, scores - high], axis=0).astype(BF16)
        parts = dot(both, sv[:, cols], 1, 0)
        raw = parts[0:8] + parts[8:16]
        raw = raw + jnp.sum(query * k8[:, cols], axis=1, keepdims=True) * v8[:, cols]
        raw = raw + jnp.sum(query * k8s[:, cols], axis=1, keepdims=True) * v8s[:, cols]
        raw_out[:, cols] = raw
        return carry

    lax.fori_loop(0, 16, suffix, 0)

    for copy in y_copies:
        copy.wait_recv()
    before = jnp.zeros((D, D), F32)
    total = jnp.zeros((D, D), F32)
    for j in range(NY):
        before = before + jnp.where(j < y, yrecv[j], 0.0)
        total = total + yrecv[j]
    high = total.astype(BF16)
    low = (total - high.astype(F32)).astype(BF16)
    asked = recv1[:, D : D + 16, :].reshape(NZ * 16, D).astype(BF16)
    told = dot(asked, high, 1, 0) + dot(asked, low, 1, 0)
    for j in range(NZ):
        send3[j, 0:D, :] = before
        send3[j, D : D + 16, :] = told[16 * j : 16 * (j + 1), :]
        before = before + recv1[j, 0:D, :]
    b_copies = {}
    for d in FAR_FIRST:
        b_copies[d] = send(
            send3.at[lax.rem(z + d, NZ)], recv3.at[z], b_s.at[d], b_r.at[d], away("sz", d)
        )
        b_copies[d].start()
    recv3[z] = send3[z]

    lax.fori_loop(10, 16, intra, 0)

    acc[...] = jnp.zeros_like(acc)

    def inter(h, prior):
        cols = lanes(h)
        low = prior.astype(BF16)
        for t in range(0, 512, 256):
            new = att[t : t + 256, cols] + dot(q[t : t + 256, cols], low, 1, 0)
            acc[t : t + 256, :] += new * new
            attb[t : t + 256, cols] = new.astype(BF16)

    f_copies = []
    for n, d in enumerate((0, *NEAR_FIRST)):
        if d:
            b_copies[d].wait_recv()
        i = lax.rem(z + NZ - d, NZ)
        state = recv3[i, 0:D, :]
        fwd[i, 0:D, :] = state + jnp.where(c == 0, own[i], 0.0)
        fwd[i, D : D + 16, :] = recv3[i, D : D + 16, :]
        copy = send(fwd.at[i], frecv.at[i], f_s.at[n], f_r.at[n], partner)
        copy.start()
        f_copies.append(copy)
        inter(c * NZ + i, state + jnp.where(c == 1, xrecv[i, 0:D, :], 0.0))
        cols = lanes(c * NZ + i)
        raw_out[:, cols] = raw_out[:, cols] + recv3[i, D : D + 8, :]
    outs = [pltpu.make_async_copy(attb.at[:, mine], att_out.at[:, mine], out_sem.at[0])]
    outs[0].start()
    for n, d in enumerate((0, *NEAR_FIRST)):
        f_copies[n].wait_recv()
        i = lax.rem(z + NZ - d, NZ)
        inter(other * NZ + i, frecv[i, 0:D, :])
        cols = lanes(other * NZ + i)
        raw_out[:, cols] = raw_out[:, cols] + frecv[i, D + 8 : D + 16, :]
    outs.append(pltpu.make_async_copy(attb.at[:, theirs], att_out.at[:, theirs], out_sem.at[1]))
    outs[1].start()

    msg[:, 0:512] = lax.dot_general(
        jnp.ones((8, D), F32),
        acc[...],
        (((1,), (1,)), ((), ())),
        precision=lax.Precision.HIGHEST,
        preferred_element_type=F32,
    )
    squares = jnp.zeros((8, D), F32)
    for h in range(16):
        piece = raw_out[:, h * D : (h + 1) * D]
        squares = squares + piece * piece
    msg[:, 512:640] = jnp.broadcast_to(jnp.sum(squares, axis=1, keepdims=True), (8, D))
    g_copies = []
    for d in (2, 1, 3):
        copy = send(msg, mrecv.at[x], g_s.at[d], g_r.at[d], away("head", d))
        copy.start()
        g_copies.append(copy)
    mrecv[x] = msg[...]
    for copy in g_copies:
        copy.wait_recv()
    sums_out[...] = (mrecv[0] + mrecv[1]) + (mrecv[2] + mrecv[3])
    for copy in outs:
        copy.wait()
    for copy in (*x_copies, *a_copies.values(), *y_copies, *b_copies.values(), *f_copies, *g_copies):
        copy.wait_send()


def scale_kernel(att, sums, last, raw, gain, out, dec):
    total = jnp.broadcast_to(sums[0:1, :], (D, D)).T
    scale = lax.rsqrt(total / 8192.0 + 1e-06)
    for h in range(16):
        cols = slice(h * D, (h + 1) * D)
        out[:, cols] = (att[:, cols].astype(F32) * scale * gain[:, cols]).astype(BF16)

    @pl.when(pl.program_id(0) == 0)
    def _():
        steps = lax.rsqrt(last[:, 0:1] / 8192.0 + 1e-06)
        value = (raw[...] * steps * gain[...]).astype(BF16)
        dec[0] = value[0:4]
        dec[1] = value[4:8]


def on_device(q, k, v, sk, sv, lengths, tq, tk, tv, gain):
    rows, width = q.shape
    sk = sk.reshape(-1, width)
    sv = sv.reshape(-1, width)
    anywhere = pl.BlockSpec(memory_space=pl.ANY)
    vmem = pl.BlockSpec(memory_space=pltpu.VMEM)
    dma = pltpu.SemaphoreType.DMA
    steps = tq.shape

    def f32(*shape):
        return pltpu.VMEM(shape, F32)

    def bf16(*shape):
        return pltpu.VMEM(shape, BF16)

    att, sums, raw = pl.pallas_call(
        main_kernel,
        out_shape=(
            jax.ShapeDtypeStruct((rows, width), BF16),
            jax.ShapeDtypeStruct((8, 640), F32),
            jax.ShapeDtypeStruct((8, width), F32),
        ),
        in_specs=[pl.BlockSpec(memory_space=pltpu.SMEM)] + [anywhere] * 8,
        out_specs=(anywhere, vmem, vmem),
        scratch_shapes=[
            *[bf16(rows, width) for _ in range(5)],
            *[bf16(*steps) for _ in range(3)],
            *[f32(8, width) for _ in range(5)],
            f32(8, 512),
            f32(rows, width),
            bf16(rows, width),
            f32(rows, D),
            f32(NZ, D, D),
            f32(NZ, D + 8, D),
            f32(NZ, D + 8, D),
            f32(NZ, D + 16, D),
            f32(NZ, D + 16, D),
            f32(D, D),
            f32(NY, D, D),
            f32(NZ, D + 16, D),
            f32(NZ, D + 16, D),
            f32(NZ, D + 16, D),
            f32(NZ, D + 16, D),
            f32(8, 640),
            f32(NX, 8, 640),
            dma((10,)),
            dma((2,)),
            *[dma((8,)) for _ in range(4)],
            *[dma((4,)) for _ in range(2)],
            *[dma((8,)) for _ in range(4)],
            *[dma((4,)) for _ in range(2)],
        ],
        compiler_params=pltpu.CompilerParams(
            collective_id=0, has_side_effects=True, vmem_limit_bytes=60 << 20
        ),
        name="main",
    )(lengths, q, k, v, sk, sv, tq, tk, tv)

    blocks = rows // D
    return pl.pallas_call(
        scale_kernel,
        grid=(blocks,),
        out_shape=(jax.ShapeDtypeStruct((rows, width), BF16), jax.ShapeDtypeStruct(steps, BF16)),
        in_specs=[
            pl.BlockSpec((D, width), lambda i: (i, 0)),
            pl.BlockSpec((8, D), lambda i: (0, i)),
            pl.BlockSpec((8, D), lambda i: (0, blocks)),
            pl.BlockSpec((8, width), lambda i: (0, 0)),
            pl.BlockSpec((1, width), lambda i: (0, 0)),
        ],
        out_specs=(
            pl.BlockSpec((D, width), lambda i: (i, 0)),
            pl.BlockSpec(steps, lambda i: (0, 0, 0)),
        ),
        compiler_params=pltpu.CompilerParams(dimension_semantics=("arbitrary",)),
        name="scale",
    )(att, sums, sums, raw, gain.reshape(1, width))


def solution(mesh):
    finer = Mesh(mesh.devices.reshape(NY, NZ, 2, NX), (*SEQ, "head"))
    return jax.shard_map(
        on_device,
        mesh=finer,
        in_specs=(
            P(SEQ, "head"),
            P(SEQ, "head"),
            P(SEQ, "head"),
            P(SEQ, None, "head"),
            P(SEQ, None, "head"),
            P(SEQ),
            P(None, SEQ, "head"),
            P(None, SEQ, "head"),
            P(None, SEQ, "head"),
            P("head"),
        ),
        out_specs=(P(SEQ, "head"), P(None, SEQ, "head")),
        check_vma=False,
    )
```

```python
import jax
import jax.numpy as jnp
from jax import lax
from jax.experimental import pallas as pl
from jax.experimental.pallas import tpu as pltpu
from jax.sharding import Mesh
from jax.sharding import PartitionSpec as P

D = 128
NY, NZ, NX = 4, 8, 4
AXES = {"sy": NY, "sz": NZ, "sc": 2, "head": NX}
SEQ = ("sy", "sz", "sc")
MESH = pl.DeviceIdType.MESH
F32 = jnp.float32
BF16 = jnp.bfloat16
CHUNKS = 4
MAIN_VMEM = 36 << 20
FAR_FIRST = (4, 3, 5, 2, 6, 1, 7)


def dot(a, b, ca, cb):
    return lax.dot_general(a, b, (((ca,), (cb,)), ((), ())), preferred_element_type=F32)


def away(axis, step):
    size = AXES[axis]
    return {axis: lax.rem(lax.axis_index(axis) + step, size)}


def lanes(head):
    return pl.ds(pl.multiple_of(head * D, D), D)


def main_kernel(
    len_ref, q_hbm, k_hbm, v_hbm, sk_hbm, sv_hbm, tq_hbm, tk_hbm, tv_hbm,
    att_out, sums_out, raw_out,
    q, k, v, sk, sv, tq, tk, tv, q8, k8, v8, k8s, v8s, mask,
    att, attb, acc, own, xsend, xrecv, chip, recv1, rsend, yrecv, send3, recv3,
    fwd, frecv, final, msg, mrecv,
    ld, out_sem, x_s, x_r, a_s, a_r, y_s, y_r, b_s, b_r, f_s, f_r, g_s, g_r,
):
    y, z, c, x = (lax.axis_index(a) for a in ("sy", "sz", "sc", "head"))
    other = 1 - c
    partner = {"sc": other}
    barrier = pltpu.get_barrier_semaphore()
    peers = [partner]
    peers += [away("sz", d) for d in range(1, NZ)]
    peers += [away("sy", d) for d in range(1, NY)]
    peers += [away("head", d) for d in range(1, NX)]
    for peer in peers:
        pl.semaphore_signal(barrier, inc=1, device_id=peer, device_id_type=MESH)

    quarter = NZ * D // 2

    def part_of(core, n):
        return pl.ds(pl.multiple_of((2 * core + n) * quarter, quarter), quarter)

    loads = []
    for core in (other, c):
        for n in range(2):
            cols = part_of(core, n)
            loads.append((k_hbm.at[:, cols], k.at[:, cols]))
            loads.append((v_hbm.at[:, cols], v.at[:, cols]))
        if core is other:
            loads.append((tq_hbm, tq))
    loads += [(q_hbm, q), (tk_hbm, tk), (tv_hbm, tv), (sk_hbm, sk), (sv_hbm, sv)]
    loads = [pltpu.make_async_copy(src, dst, ld.at[n]) for n, (src, dst) in enumerate(loads)]
    for copy in loads:
        copy.start()

    def send(src, dst, s, r, peer):
        copy = pltpu.make_async_remote_copy(
            src_ref=src, dst_ref=dst, send_sem=s, recv_sem=r, device_id=peer, device_id_type=MESH
        )
        return copy

    def their_state(i, carry):
        cols = lanes(other * NZ + i)
        xsend[i, 0:D, :] = dot(k[:, cols], v[:, cols], 0, 0)
        return carry

    for n in range(2):
        loads[2 * n].wait()
        loads[2 * n + 1].wait()
        lax.fori_loop(4 * n, 4 * n + 4, their_state, 0, unroll=4)
    loads[4].wait()
    q8[0:4, :] = tq[0].astype(F32)
    q8[4:8, :] = tq[1].astype(F32)
    for i in range(NZ):
        xsend[i, D : D + 8, :] = q8[:, lanes(other * NZ + i)]
    pl.semaphore_wait(barrier, len(peers))
    x_copies = []
    for i in range(NZ):
        copy = send(xsend.at[i], xrecv.at[i], x_s.at[i], x_r.at[i], partner)
        copy.start()
        x_copies.append(copy)

    def my_state(i, carry):
        cols = lanes(c * NZ + i)
        own[i] = dot(k[:, cols], v[:, cols], 0, 0)
        return carry

    for n in range(2):
        loads[5 + 2 * n].wait()
        loads[6 + 2 * n].wait()
        lax.fori_loop(4 * n, 4 * n + 4, my_state, 0, unroll=4)
    for copy in x_copies:
        copy.wait_recv()

    def chip_sum(i, dst):
        dst[0:D, :] = own[i] + xrecv[i, 0:D, :]
        dst[D : D + 8, :] = q8[:, lanes(c * NZ + i)]
        dst[D + 8 : D + 16, :] = xrecv[i, D : D + 8, :]

    def span(j):
        first = j * D // CHUNKS
        return pl.ds(first, (D + 16 if j == CHUNKS - 1 else first + D // CHUNKS) - first)

    for d in range(1, NZ):
        i = lax.rem(z + d, NZ)
        chip_sum(i, chip.at[i])
    a_copies = {}
    for j in range(CHUNKS):
        for d in FAR_FIRST:
            i = lax.rem(z + d, NZ)
            a_copies[j, d] = send(
                chip.at[i, span(j)],
                recv1.at[z, span(j)],
                a_s.at[j, d],
                a_r.at[j, d],
                away("sz", d),
            )
            a_copies[j, d].start()
    chip_sum(z, recv1.at[z])

    rows = lax.broadcasted_iota(jnp.int32, (256, 256), 0)
    columns = lax.broadcasted_iota(jnp.int32, (256, 256), 1)
    causal = columns <= rows

    def intra(h, carry):
        cols = lanes(h)
        top, bottom = q[0:256, cols], q[256:512, cols]
        s00 = jnp.where(causal, dot(top, k[0:256, cols], 1, 1), 0.0).astype(BF16)
        att[0:256, cols] = dot(s00, v[0:256, cols], 1, 0)
        s10 = dot(bottom, k[0:256, cols], 1, 1).astype(BF16)
        s11 = jnp.where(causal, dot(bottom, k[256:512, cols], 1, 1), 0.0).astype(BF16)
        att[256:512, cols] = dot(s10, v[0:256, cols], 1, 0) + dot(s11, v[256:512, cols], 1, 0)
        return carry

    def row_sum(j):
        part = slice(j * D // CHUNKS, (j + 1) * D // CHUNKS)
        for d in FAR_FIRST:
            a_copies[j, d].wait_recv()
        total = recv1[0, part, :]
        for n in range(1, NZ):
            total = total + recv1[n, part, :]
        rsend[part, :] = total
        yrecv[y, part, :] = total
        for d in (2, 1, 3):
            copy = send(
                rsend.at[part], yrecv.at[y, part], y_s.at[j, d], y_r.at[j, d], away("sy", d)
            )
            copy.start()
            y_copies[j, d] = copy

    def ready_steps():
        for copy in loads[10:]:
            copy.wait()
        k8[0:4, :] = tk[0].astype(F32)
        k8[4:8, :] = tk[1].astype(F32)
        v8[0:4, :] = tv[0].astype(F32)
        v8[4:8, :] = tv[1].astype(F32)
        k8s[...] = jnp.zeros_like(k8s)
        v8s[...] = jnp.zeros_like(v8s)
        k8s[4:8, :] = tk[0].astype(F32)
        v8s[4:8, :] = tv[0].astype(F32)
        row = lax.rem(lax.broadcasted_iota(jnp.int32, (8, D), 0), 4)
        column = lax.broadcasted_iota(jnp.int32, (8, D), 1)
        for n in range(4):
            live = (row == n) & (column < len_ref[n])
            mask[:, n * D : (n + 1) * D] = jnp.where(live, 1.0, 0.0)

    def suffix(h, carry):
        cols = lanes(h)
        query = q8[:, cols]
        scores = dot(query.astype(BF16), sk[:, cols], 1, 1) * mask[...]
        high = scores.astype(BF16).astype(F32)
        both = jnp.concatenate([high, scores - high], axis=0).astype(BF16)
        parts = dot(both, sv[:, cols], 1, 0)
        raw = parts[0:8] + parts[8:16]
        raw = raw + jnp.sum(query * k8[:, cols], axis=1, keepdims=True) * v8[:, cols]
        raw = raw + jnp.sum(query * k8s[:, cols], axis=1, keepdims=True) * v8s[:, cols]
        raw_out[:, cols] = raw
        return carry

    def priors(j):
        part = slice(j * D // CHUNKS, (j + 1) * D // CHUNKS)
        for d in (2, 1, 3):
            y_copies[j, d].wait_recv()
        before = jnp.zeros((D // CHUNKS, D), F32)
        total = jnp.zeros((D // CHUNKS, D), F32)
        for n in range(NY):
            before = before + jnp.where(n < y, yrecv[n, part, :], 0.0)
            total = total + yrecv[n, part, :]
        final[part, :] = total
        for n in range(NZ):
            send3[n, part, :] = before
            before = before + recv1[n, part, :]
        if j == CHUNKS - 1:
            high = final[...].astype(BF16)
            low = (final[...] - high.astype(F32)).astype(BF16)
            asked = recv1[:, D : D + 16, :].reshape(NZ * 16, D).astype(BF16)
            told = dot(asked, high, 1, 0) + dot(asked, low, 1, 0)
            for n in range(NZ):
                send3[n, D : D + 16, :] = told[16 * n : 16 * (n + 1), :]
        for d in FAR_FIRST:
            b_copies[j, d] = send(
                send3.at[lax.rem(z + d, NZ), span(j)],
                recv3.at[z, span(j)],
                b_s.at[j, d],
                b_r.at[j, d],
                away("sz", d),
            )
            b_copies[j, d].start()

    y_copies, b_copies = {}, {}
    loads[9].wait()
    lax.fori_loop(0, 12, intra, 0, unroll=2)
    row_sum(0)
    lax.fori_loop(12, 16, intra, 0, unroll=2)
    row_sum(1)
    ready_steps()
    lax.fori_loop(0, 4, suffix, 0, unroll=2)
    priors(0)
    row_sum(2)
    lax.fori_loop(4, 10, suffix, 0, unroll=2)
    priors(1)
    row_sum(3)
    lax.fori_loop(10, 16, suffix, 0, unroll=2)
    priors(2)
    priors(3)
    recv3[z] = send3[z]

    acc[...] = jnp.zeros_like(acc)

    def inter(h, prior):
        cols = lanes(h)
        low = prior.astype(BF16)
        for t in range(0, 512, 256):
            new = att[t : t + 256, cols] + dot(q[t : t + 256, cols], low, 1, 0)
            acc[t : t + 256, :] += new * new
            attb[t : t + 256, cols] = new.astype(BF16)

    f_copies = []
    order = (0, *FAR_FIRST)

    def direct(n):
        d = order[n]
        if d:
            for j in range(CHUNKS):
                b_copies[j, d].wait_recv()
        i = lax.rem(z + NZ - d, NZ)
        state = recv3[i, 0:D, :]
        fwd[i, 0:D, :] = state + jnp.where(c == 0, own[i], 0.0)
        fwd[i, D : D + 16, :] = recv3[i, D : D + 16, :]
        copy = send(fwd.at[i], frecv.at[i], f_s.at[n], f_r.at[n], partner)
        copy.start()
        f_copies.append(copy)
        inter(c * NZ + i, state + jnp.where(c == 1, xrecv[i, 0:D, :], 0.0))
        cols = lanes(c * NZ + i)
        raw_out[:, cols] = raw_out[:, cols] + recv3[i, D : D + 8, :]

    def forwarded(n):
        f_copies[n].wait_recv()
        i = lax.rem(z + NZ - order[n], NZ)
        inter(other * NZ + i, frecv[i, 0:D, :])
        cols = lanes(other * NZ + i)
        raw_out[:, cols] = raw_out[:, cols] + frecv[i, D + 8 : D + 16, :]

    for n in range(NZ):
        direct(n)
        if n > 1:
            forwarded(n - 2)
    for n in range(NZ - 2, NZ):
        forwarded(n)
    outs = [pltpu.make_async_copy(attb, att_out, out_sem.at[0])]
    outs[0].start()

    msg[:, 0:512] = lax.dot_general(
        jnp.ones((8, D), F32),
        acc[...],
        (((1,), (1,)), ((), ())),
        precision=lax.Precision.HIGHEST,
        preferred_element_type=F32,
    )
    squares = jnp.zeros((8, D), F32)
    for h in range(16):
        piece = raw_out[:, h * D : (h + 1) * D]
        squares = squares + piece * piece
    msg[:, 512:640] = jnp.broadcast_to(jnp.sum(squares, axis=1, keepdims=True), (8, D))
    g_copies = []
    for d in (2, 1, 3):
        copy = send(msg, mrecv.at[x], g_s.at[d], g_r.at[d], away("head", d))
        copy.start()
        g_copies.append(copy)
    mrecv[x] = msg[...]
    for copy in g_copies:
        copy.wait_recv()
    sums_out[...] = (mrecv[0] + mrecv[1]) + (mrecv[2] + mrecv[3])
    for copy in outs:
        copy.wait()
    for copy in (*x_copies, *a_copies.values(), *y_copies.values(), *b_copies.values(), *f_copies, *g_copies):
        copy.wait_send()


def scale_kernel(att, sums, last, raw, gain, out, dec):
    total = jnp.broadcast_to(sums[0:1, :], (D, D)).T
    scale = lax.rsqrt(total / 8192.0 + 1e-06)
    for h in range(16):
        cols = slice(h * D, (h + 1) * D)
        out[:, cols] = (att[:, cols].astype(F32) * scale * gain[:, cols]).astype(BF16)

    @pl.when(pl.program_id(0) == 0)
    def _():
        steps = lax.rsqrt(last[:, 0:1] / 8192.0 + 1e-06)
        value = (raw[...] * steps * gain[...]).astype(BF16)
        dec[0] = value[0:4]
        dec[1] = value[4:8]


def on_device(q, k, v, sk, sv, lengths, tq, tk, tv, gain):
    rows, width = q.shape
    sk = sk.reshape(-1, width)
    sv = sv.reshape(-1, width)
    anywhere = pl.BlockSpec(memory_space=pl.ANY)
    vmem = pl.BlockSpec(memory_space=pltpu.VMEM)
    dma = pltpu.SemaphoreType.DMA
    steps = tq.shape

    def f32(*shape):
        return pltpu.VMEM(shape, F32)

    def bf16(*shape):
        return pltpu.VMEM(shape, BF16)

    att, sums, raw = pl.pallas_call(
        main_kernel,
        out_shape=(
            jax.ShapeDtypeStruct((rows, width), BF16),
            jax.ShapeDtypeStruct((8, 640), F32),
            jax.ShapeDtypeStruct((8, width), F32),
        ),
        in_specs=[pl.BlockSpec(memory_space=pltpu.SMEM)] + [anywhere] * 8,
        out_specs=(anywhere, vmem, vmem),
        scratch_shapes=[
            *[bf16(rows, width) for _ in range(5)],
            *[bf16(*steps) for _ in range(3)],
            *[f32(8, width) for _ in range(5)],
            f32(8, 512),
            f32(rows, width),
            bf16(rows, width),
            f32(rows, D),
            f32(NZ, D, D),
            f32(NZ, D + 8, D),
            f32(NZ, D + 8, D),
            f32(NZ, D + 16, D),
            f32(NZ, D + 16, D),
            f32(D, D),
            f32(NY, D, D),
            f32(NZ, D + 16, D),
            f32(NZ, D + 16, D),
            f32(NZ, D + 16, D),
            f32(NZ, D + 16, D),
            f32(D, D),
            f32(8, 640),
            f32(NX, 8, 640),
            dma((14,)),
            dma((1,)),
            *[dma((8,)) for _ in range(2)],
            *[dma((CHUNKS, 8)) for _ in range(2)],
            *[dma((CHUNKS, 4)) for _ in range(2)],
            *[dma((CHUNKS, 8)) for _ in range(2)],
            *[dma((8,)) for _ in range(2)],
            *[dma((4,)) for _ in range(2)],
        ],
        compiler_params=pltpu.CompilerParams(
            collective_id=0, has_side_effects=True, vmem_limit_bytes=MAIN_VMEM
        ),
        name="main",
    )(*(pltpu.with_memory_space_constraint(a, pltpu.HBM) for a in (lengths, q, k, v, sk, sv, tq, tk, tv)))

    blocks = rows // D
    return pl.pallas_call(
        scale_kernel,
        grid=(blocks,),
        out_shape=(jax.ShapeDtypeStruct((rows, width), BF16), jax.ShapeDtypeStruct(steps, BF16)),
        in_specs=[
            pl.BlockSpec((D, width), lambda i: (i, 0)),
            pl.BlockSpec((8, D), lambda i: (0, i)),
            pl.BlockSpec((8, D), lambda i: (0, blocks)),
            pl.BlockSpec((8, width), lambda i: (0, 0)),
            pl.BlockSpec((1, width), lambda i: (0, 0)),
        ],
        out_specs=(
            pl.BlockSpec((D, width), lambda i: (i, 0)),
            pl.BlockSpec(steps, lambda i: (0, 0, 0)),
        ),
        compiler_params=pltpu.CompilerParams(dimension_semantics=("arbitrary",), vmem_limit_bytes=12 << 20),
        name="scale",
    )(att, sums, sums, raw, gain.reshape(1, width))


def solution(mesh):
    finer = Mesh(mesh.devices.reshape(NY, NZ, 2, NX), (*SEQ, "head"))
    return jax.shard_map(
        on_device,
        mesh=finer,
        in_specs=(
            P(SEQ, "head"),
            P(SEQ, "head"),
            P(SEQ, "head"),
            P(SEQ, None, "head"),
            P(SEQ, None, "head"),
            P(SEQ),
            P(None, SEQ, "head"),
            P(None, SEQ, "head"),
            P(None, SEQ, "head"),
            P("head"),
        ),
        out_specs=(P(SEQ, "head"), P(None, SEQ, "head")),
        check_vma=False,
    )
```

```python
import jax
import jax.numpy as jnp
from jax import lax
from jax.experimental import pallas as pl
from jax.experimental.pallas import tpu as pltpu
from jax.sharding import Mesh
from jax.sharding import PartitionSpec as P

D = 128
NY, NZ, NX = 4, 8, 4
AXES = {"sy": NY, "sz": NZ, "sc": 2, "head": NX}
SEQ = ("sy", "sz", "sc")
MESH = pl.DeviceIdType.MESH
F32 = jnp.float32
BF16 = jnp.bfloat16
CHUNKS = 4
MAIN_VMEM = 36 << 20
FAR_FIRST = (4, 3, 5, 2, 6, 1, 7)
WAIT_ORDER = (1, 7, 2, 6, 3, 5, 4)
PLAN = (
    ("intra", 0, 12),
    ("sum", 0),
    ("intra", 12, 16),
    ("sum", 1),
    ("steps",),
    ("suffix", 0, 4),
    ("prior", 0),
    ("sum", 2),
    ("suffix", 4, 10),
    ("prior", 1),
    ("suffix", 10, 16),
    ("sum", 3),
    ("prior", 2),
    ("prior", 3),
    ("answers",),
)


def dot(a, b, ca, cb):
    return lax.dot_general(a, b, (((ca,), (cb,)), ((), ())), preferred_element_type=F32)


def away(axis, step):
    size = AXES[axis]
    return {axis: lax.rem(lax.axis_index(axis) + step, size)}


def lanes(head):
    return pl.ds(pl.multiple_of(head * D, D), D)


def main_kernel(
    len_hbm, q_hbm, k_hbm, v_hbm, sk_hbm, sv_hbm, tq_hbm, tk_hbm, tv_hbm,
    att_out, sums_out, raw_hbm,
    len_ref, raw_out,
    q, k, v, sk, sv, tq, tk, tv, q8, k8, v8, k8s, v8s, mask,
    att, attb, acc, own, xsend, xrecv, chip, recv1, rsend, yrecv, send3, recv3,
    qrecv, fwd, frecv, rest, frest, final, msg,
    ld, out_sem, x_s, x_r, q_s, q_r, a_s, a_r, y_s, y_r, b_s, b_r, f_s, f_r, g_s, g_r,
):
    y, z, c, x = (lax.axis_index(a) for a in ("sy", "sz", "sc", "head"))
    other = 1 - c
    partner = {"sc": other}
    barrier = pltpu.get_barrier_semaphore()
    peers = [partner]
    peers += [away("sz", d) for d in range(1, NZ)]
    peers += [away("sz", d) | partner for d in range(1, NZ)]
    peers += [away("sy", d) for d in range(1, NY)]
    peers += [away("head", d) for d in range(1, NX)]
    for peer in peers:
        pl.semaphore_signal(barrier, inc=1, device_id=peer, device_id_type=MESH)

    quarter = NZ * D // 2

    def part_of(core, n):
        return pl.ds(pl.multiple_of((2 * core + n) * quarter, quarter), quarter)

    loads = []
    for n in range(2):
        for core in (other, c):
            cols = part_of(core, n)
            loads.append((k_hbm.at[:, cols], k.at[:, cols]))
            loads.append((v_hbm.at[:, cols], v.at[:, cols]))
        if n == 0:
            loads.append((tq_hbm, tq))
    loads += [(q_hbm, q), (len_hbm, len_ref), (tk_hbm, tk), (tv_hbm, tv), (sk_hbm, sk), (sv_hbm, sv)]
    loads = [pltpu.make_async_copy(src, dst, ld.at[n]) for n, (src, dst) in enumerate(loads)]
    for copy in loads:
        copy.start()

    def send(src, dst, s, r, peer):
        copy = pltpu.make_async_remote_copy(
            src_ref=src, dst_ref=dst, send_sem=s, recv_sem=r, device_id=peer, device_id_type=MESH
        )
        return copy

    def wait_bytes(ref, sem):
        pltpu.make_async_copy(ref, ref, sem).wait()

    def their_state(i, carry):
        cols = lanes(other * NZ + i)
        xsend[i] = dot(k[:, cols], v[:, cols], 0, 0)
        return carry

    def my_state(i, carry):
        cols = lanes(c * NZ + i)
        own[i] = dot(k[:, cols], v[:, cols], 0, 0)
        return carry

    def exchange(n):
        for i in range(4 * n, 4 * n + 4):
            send(xsend.at[i], xrecv.at[i], x_s, x_r, partner).start()

    loads[0].wait()
    loads[1].wait()
    lax.fori_loop(0, 4, their_state, 0, unroll=4)
    loads[4].wait()
    q8[0:4, :] = tq[0].astype(F32)
    q8[4:8, :] = tq[1].astype(F32)
    pl.semaphore_wait(barrier, len(peers))
    exchange(0)
    for d in (4, 3, 5, 2, 6, 1, 7, 0):
        for e in range(2):
            if d or e:
                core = other if e else c
                i = lax.rem(z + d, NZ)
                asking = q8.at[:, lanes(core * NZ + i)]
                send(asking, qrecv.at[z, c], q_s, q_r, {"sz": i, "sc": core}).start()
    qrecv[z, c] = q8[:, lanes(c * NZ + z)]
    loads[2].wait()
    loads[3].wait()
    lax.fori_loop(0, 4, my_state, 0, unroll=4)
    loads[5].wait()
    loads[6].wait()
    lax.fori_loop(4, 8, their_state, 0, unroll=4)
    exchange(1)
    loads[7].wait()
    loads[8].wait()
    lax.fori_loop(4, 8, my_state, 0, unroll=4)
    wait_bytes(xrecv, x_r)

    def chip_sum(i, dst):
        dst[...] = own[i] + xrecv[i]

    def span(j):
        first = j * D // CHUNKS
        return pl.ds(first, 16 if j == CHUNKS else D // CHUNKS)

    for d in range(1, NZ):
        i = lax.rem(z + d, NZ)
        chip_sum(i, chip.at[i])
    for j in range(CHUNKS):
        for d in FAR_FIRST:
            i = lax.rem(z + d, NZ)
            send(chip.at[i, span(j)], recv1.at[z, span(j)], a_s, a_r.at[j], {"sz": i}).start()
    chip_sum(z, recv1.at[z])

    rows = lax.broadcasted_iota(jnp.int32, (256, 256), 0)
    columns = lax.broadcasted_iota(jnp.int32, (256, 256), 1)
    causal = columns <= rows

    def intra(h, carry):
        cols = lanes(h)
        top, bottom = q[0:256, cols], q[256:512, cols]
        s00 = jnp.where(causal, dot(top, k[0:256, cols], 1, 1), 0.0).astype(BF16)
        att[0:256, cols] = dot(s00, v[0:256, cols], 1, 0)
        s10 = dot(bottom, k[0:256, cols], 1, 1).astype(BF16)
        s11 = jnp.where(causal, dot(bottom, k[256:512, cols], 1, 1), 0.0).astype(BF16)
        att[256:512, cols] = dot(s10, v[0:256, cols], 1, 0) + dot(s11, v[256:512, cols], 1, 0)
        return carry

    def row_sum(j):
        part = slice(j * D // CHUNKS, (j + 1) * D // CHUNKS)
        wait_bytes(recv1.at[0 : NZ - 1, part], a_r.at[j])
        total = recv1[0, part, :]
        for n in range(1, NZ):
            total = total + recv1[n, part, :]
        rsend[part, :] = total
        yrecv[y, part, :] = total
        for d in (2, 1, 3):
            send(rsend.at[part], yrecv.at[y, part], y_s, y_r.at[j], away("sy", d)).start()

    def ready_steps():
        for copy in loads[10:]:
            copy.wait()
        k8[0:4, :] = tk[0].astype(F32)
        k8[4:8, :] = tk[1].astype(F32)
        v8[0:4, :] = tv[0].astype(F32)
        v8[4:8, :] = tv[1].astype(F32)
        k8s[...] = jnp.zeros_like(k8s)
        v8s[...] = jnp.zeros_like(v8s)
        k8s[4:8, :] = tk[0].astype(F32)
        v8s[4:8, :] = tv[0].astype(F32)
        row = lax.rem(lax.broadcasted_iota(jnp.int32, (8, D), 0), 4)
        column = lax.broadcasted_iota(jnp.int32, (8, D), 1)
        for n in range(4):
            live = (row == n) & (column < len_ref[n])
            mask[:, n * D : (n + 1) * D] = jnp.where(live, 1.0, 0.0)

    def suffix(h, carry):
        cols = lanes(h)
        query = q8[:, cols]
        scores = dot(query.astype(BF16), sk[:, cols], 1, 1) * mask[...]
        high = scores.astype(BF16).astype(F32)
        both = jnp.concatenate([high, scores - high], axis=0).astype(BF16)
        parts = dot(both, sv[:, cols], 1, 0)
        raw = parts[0:8] + parts[8:16]
        raw = raw + jnp.sum(query * k8[:, cols], axis=1, keepdims=True) * v8[:, cols]
        raw = raw + jnp.sum(query * k8s[:, cols], axis=1, keepdims=True) * v8s[:, cols]
        raw_out[:, cols] = raw
        return carry

    def priors(j):
        part = slice(j * D // CHUNKS, (j + 1) * D // CHUNKS)
        wait_bytes(yrecv.at[0 : NY - 1, part], y_r.at[j])
        before = jnp.zeros((D // CHUNKS, D), F32)
        total = jnp.zeros((D // CHUNKS, D), F32)
        for n in range(NY):
            before = before + jnp.where(n < y, yrecv[n, part, :], 0.0)
            total = total + yrecv[n, part, :]
        final[part, :] = total
        for n in range(NZ):
            send3[n, part, :] = before
            before = before + recv1[n, part, :]
        ship(j)
        recv3[z, part, :] = send3[z, part, :]

    def ship(j):
        for d in FAR_FIRST:
            i = lax.rem(z + d, NZ)
            sem = b_r.at[0 if j == CHUNKS else d]
            send(send3.at[i, span(j)], recv3.at[z, span(j)], b_s, sem, {"sz": i}).start()

    def answers():
        wait_bytes(q8.at[:, 0 : 15 * D], q_r)
        high = final[...].astype(BF16)
        low = (final[...] - high.astype(F32)).astype(BF16)
        asked = qrecv[...].reshape(NZ * 16, D).astype(BF16)
        told = dot(asked, high, 1, 0) + dot(asked, low, 1, 0)
        for n in range(NZ):
            send3[n, D : D + 16, :] = told[16 * n : 16 * (n + 1), :]
        ship(CHUNKS)
        recv3[z, D : D + 16, :] = send3[z, D : D + 16, :]

    loads[9].wait()
    work = {
        "intra": lambda a, b: lax.fori_loop(a, b, intra, 0, unroll=2),
        "suffix": lambda a, b: lax.fori_loop(a, b, suffix, 0, unroll=2),
        "steps": ready_steps,
        "sum": row_sum,
        "prior": priors,
        "answers": answers,
    }
    for name, *args in PLAN:
        work[name](*args)

    acc[...] = jnp.zeros_like(acc)

    def inter(h, prior):
        cols = lanes(h)
        low = prior.astype(BF16)
        for t in range(0, 512, 256):
            new = att[t : t + 256, cols] + dot(q[t : t + 256, cols], low, 1, 0)
            acc[t : t + 256, :] += new * new
            attb[t : t + 256, cols] = new.astype(BF16)

    for d in (0, *WAIT_ORDER):
        i = lax.rem(z + NZ - d, NZ)
        if d:
            wait_bytes(recv3.at[i, 0:D], b_r.at[d])
        fwd[i] = recv3[i, 0:D, :] + jnp.where(c == 0, own[i], 0.0)
        send(fwd.at[i], frecv.at[i], f_s.at[0], f_r.at[0], partner).start()

    def own_inter(i, carry):
        inter(c * NZ + i, recv3[i, 0:D, :] + jnp.where(c == 1, xrecv[i], 0.0))
        return carry

    def their_inter(i, carry):
        inter(other * NZ + i, frecv[i])
        return carry

    lax.fori_loop(0, NZ, own_inter, 0, unroll=4)
    wait_bytes(recv3.at[0 : NZ - 1, D : D + 16], b_r.at[0])
    for i in range(NZ):
        rest[i] = recv3[i, pl.ds(pl.multiple_of(D + 8 * other, 8), 8), :]
    send(rest, frest, f_s.at[1], f_r.at[1], partner).start()
    wait_bytes(frecv, f_r.at[0])
    lax.fori_loop(0, NZ, their_inter, 0, unroll=4)
    wait_bytes(frest, f_r.at[1])
    for i in range(NZ):
        cols = lanes(c * NZ + i)
        mine = recv3[i, pl.ds(pl.multiple_of(D + 8 * c, 8), 8), :]
        raw_out[:, cols] = raw_out[:, cols] + mine
        cols = lanes(other * NZ + i)
        raw_out[:, cols] = raw_out[:, cols] + frest[i]
    outs = [pltpu.make_async_copy(attb, att_out, out_sem.at[0])]
    outs[0].start()
    outs.append(pltpu.make_async_copy(raw_out, raw_hbm, out_sem.at[1]))
    outs[1].start()

    squares = lax.dot_general(
        jnp.ones((8, D), F32),
        acc[...],
        (((1,), (1,)), ((), ())),
        precision=lax.Precision.HIGHEST,
        preferred_element_type=F32,
    )
    for n in range(4):
        msg[n : n + 1, :] = squares[0:1, n * D : (n + 1) * D]
        msg[n + 4 : n + 5, :] = squares[0:1, n * D : (n + 1) * D]
    squares = jnp.zeros((8, D), F32)
    for h in range(16):
        piece = raw_out[:, h * D : (h + 1) * D]
        squares = squares + piece * piece
    msg[8:16, :] = jnp.broadcast_to(jnp.sum(squares, axis=1, keepdims=True), (8, D))
    for d in (2, 1, 3):
        send(msg, sums_out.at[x], g_s, g_r, away("head", d)).start()
    outs.append(pltpu.make_async_copy(msg, sums_out.at[x], out_sem.at[2]))
    outs[2].start()
    wait_bytes(xsend, x_s)
    wait_bytes(q8.at[:, 0 : 15 * D], q_s)
    wait_bytes(chip.at[0 : NZ - 1], a_s)
    wait_bytes(yrecv.at[0 : NY - 1], y_s)
    wait_bytes(send3.at[0 : NZ - 1], b_s)
    wait_bytes(fwd, f_s.at[0])
    wait_bytes(rest, f_s.at[1])
    wait_bytes(sums_out.at[0 : NX - 1], g_s)
    wait_bytes(sums_out.at[0 : NX - 1], g_r)
    for copy in outs:
        copy.wait()


def scale_kernel(att, sums, raw, gain, out, dec):
    row = pl.ds(pl.program_id(0), 1)
    total = (sums[0, row, :] + sums[1, row, :]) + (sums[2, row, :] + sums[3, row, :])
    total = jnp.broadcast_to(total, (D, D)).T
    scale = lax.rsqrt(total / 8192.0 + 1e-06)
    for h in range(16):
        cols = slice(h * D, (h + 1) * D)
        out[:, cols] = (att[:, cols].astype(F32) * scale * gain[:, cols]).astype(BF16)

    @pl.when(pl.program_id(0) == 0)
    def _():
        steps = (sums[0, 8:16, 0:1] + sums[1, 8:16, 0:1]) + (sums[2, 8:16, 0:1] + sums[3, 8:16, 0:1])
        steps = lax.rsqrt(steps / 8192.0 + 1e-06)
        value = (raw[...] * steps * gain[...]).astype(BF16)
        dec[0] = value[0:4]
        dec[1] = value[4:8]


def on_device(q, k, v, sk, sv, lengths, tq, tk, tv, gain):
    rows, width = q.shape
    sk = sk.reshape(-1, width)
    sv = sv.reshape(-1, width)
    anywhere = pl.BlockSpec(memory_space=pl.ANY)
    dma = pltpu.SemaphoreType.DMA
    steps = tq.shape

    def f32(*shape):
        return pltpu.VMEM(shape, F32)

    def bf16(*shape):
        return pltpu.VMEM(shape, BF16)

    att, sums, raw = pl.pallas_call(
        main_kernel,
        out_shape=(
            jax.ShapeDtypeStruct((rows, width), BF16),
            jax.ShapeDtypeStruct((NX, 16, D), F32),
            jax.ShapeDtypeStruct((8, width), F32),
        ),
        in_specs=[anywhere] * 9,
        out_specs=(anywhere, anywhere, anywhere),
        scratch_shapes=[
            pltpu.SMEM((4,), jnp.int32),
            f32(8, width),
            *[bf16(rows, width) for _ in range(5)],
            *[bf16(*steps) for _ in range(3)],
            *[f32(8, width) for _ in range(5)],
            f32(8, 512),
            f32(rows, width),
            bf16(rows, width),
            f32(rows, D),
            f32(NZ, D, D),
            f32(NZ, D, D),
            f32(NZ, D, D),
            f32(NZ, D, D),
            f32(NZ, D, D),
            f32(D, D),
            f32(NY, D, D),
            f32(NZ, D + 16, D),
            f32(NZ, D + 16, D),
            f32(NZ, 2, 8, D),
            f32(NZ, D, D),
            f32(NZ, D, D),
            f32(NZ, 8, D),
            f32(NZ, 8, D),
            f32(D, D),
            f32(16, D),
            dma((15,)),
            dma((3,)),
            *[dma(()) for _ in range(4)],
            dma(()),
            dma((CHUNKS,)),
            dma(()),
            dma((CHUNKS,)),
            dma(()),
            dma((NZ,)),
            dma((2,)),
            dma((2,)),
            dma(()),
            dma(()),
        ],
        compiler_params=pltpu.CompilerParams(
            collective_id=0, has_side_effects=True, vmem_limit_bytes=MAIN_VMEM
        ),
        name="main",
    )(*(pltpu.with_memory_space_constraint(a, pltpu.HBM) for a in (lengths, q, k, v, sk, sv, tq, tk, tv)))

    blocks = rows // D
    return pl.pallas_call(
        scale_kernel,
        grid=(blocks,),
        out_shape=(jax.ShapeDtypeStruct((rows, width), BF16), jax.ShapeDtypeStruct(steps, BF16)),
        in_specs=[
            pl.BlockSpec((D, width), lambda i: (i, 0)),
            pl.BlockSpec((NX, 16, D), lambda i: (0, 0, 0)),
            pl.BlockSpec((8, width), lambda i: (0, 0)),
            pl.BlockSpec((1, width), lambda i: (0, 0)),
        ],
        out_specs=(
            pl.BlockSpec((D, width), lambda i: (i, 0)),
            pl.BlockSpec(steps, lambda i: (0, 0, 0)),
        ),
        compiler_params=pltpu.CompilerParams(dimension_semantics=("arbitrary",), vmem_limit_bytes=12 << 20),
        name="scale",
    )(att, sums, raw, gain.reshape(1, width))


def solution(mesh):
    finer = Mesh(mesh.devices.reshape(NY, NZ, 2, NX), (*SEQ, "head"))
    return jax.shard_map(
        on_device,
        mesh=finer,
        in_specs=(
            P(SEQ, "head"),
            P(SEQ, "head"),
            P(SEQ, "head"),
            P(SEQ, None, "head"),
            P(SEQ, None, "head"),
            P(SEQ),
            P(None, SEQ, "head"),
            P(None, SEQ, "head"),
            P(None, SEQ, "head"),
            P("head"),
        ),
        out_specs=(P(SEQ, "head"), P(None, SEQ, "head")),
        check_vma=False,
    )
```

```python
import jax
import jax.numpy as jnp
from jax import lax
from jax.experimental import pallas as pl
from jax.experimental.pallas import tpu as pltpu
from jax.sharding import Mesh
from jax.sharding import PartitionSpec as P

D = 128
NY, NZ, NX = 4, 8, 4
AXES = {"sy": NY, "sz": NZ, "sc": 2, "head": NX}
SEQ = ("sy", "sz", "sc")
MESH = pl.DeviceIdType.MESH
F32 = jnp.float32
BF16 = jnp.bfloat16
BOUNDS = (0, 32, 64, 96, 128)
CHUNKS = len(BOUNDS) - 1
MAIN_VMEM = 36 << 20
FAR_FIRST = (4, 3, 5, 2, 6, 1, 7)
WAIT_ORDER = (1, 7, 2, 6, 3, 5, 4)
PLAN = (
    ("intra", 0, 12),
    ("sum", 0),
    ("intra", 12, 16),
    ("sum", 1),
    ("steps",),
    ("suffix", 0, 4),
    ("prior", 0),
    ("sum", 2),
    ("suffix", 4, 10),
    ("prior", 1),
    ("suffix", 10, 16),
    ("sum", 3),
    ("prior", 2),
    ("prior", 3),
    ("answers",),
)


def dot(a, b, ca, cb):
    return lax.dot_general(a, b, (((ca,), (cb,)), ((), ())), preferred_element_type=F32)


def away(axis, step):
    size = AXES[axis]
    return {axis: lax.rem(lax.axis_index(axis) + step, size)}


def lanes(head):
    return pl.ds(pl.multiple_of(head * D, D), D)


def main_kernel(
    len_hbm, q_hbm, k_hbm, v_hbm, sk_hbm, sv_hbm, tq_hbm, tk_hbm, tv_hbm,
    att_out, sums_out, raw_hbm,
    len_ref, raw_out,
    q, k, v, sk, sv, tq, tk, tv, q8, k8, v8, k8s, v8s, mask,
    att, attb, acc, own, xsend, xrecv, chip, recv1, rsend, yrecv, send3, recv3,
    qrecv, fwd, frecv, tell, heard, final, msg,
    ld, out_sem, x_s, x_r, q_s, q_r, a_s, a_r, y_s, y_r, b_s, b_r, f_s, f_r, t_s, t_r, g_s, g_r,
):
    y, z, c, x = (lax.axis_index(a) for a in ("sy", "sz", "sc", "head"))
    other = 1 - c
    partner = {"sc": other}
    barrier = pltpu.get_barrier_semaphore()
    peers = [partner]
    peers += [away("sz", d) for d in range(1, NZ)]
    peers += [away("sz", d) | partner for d in range(1, NZ)]
    peers += [away("sy", d) for d in range(1, NY)]
    peers += [away("head", d) for d in range(1, NX)]
    for peer in peers:
        pl.semaphore_signal(barrier, inc=1, device_id=peer, device_id_type=MESH)

    quarter = NZ * D // 2

    def part_of(core, n):
        return pl.ds(pl.multiple_of((2 * core + n) * quarter, quarter), quarter)

    loads = []
    for core in (other, c):
        for n in range(2):
            cols = part_of(core, n)
            loads.append((k_hbm.at[:, cols], k.at[:, cols]))
            loads.append((v_hbm.at[:, cols], v.at[:, cols]))
        if core is other:
            loads.append((tq_hbm, tq))
    loads += [(q_hbm, q), (len_hbm, len_ref), (tk_hbm, tk), (tv_hbm, tv), (sk_hbm, sk), (sv_hbm, sv)]
    loads = [pltpu.make_async_copy(src, dst, ld.at[n]) for n, (src, dst) in enumerate(loads)]
    for copy in loads:
        copy.start()

    def send(src, dst, s, r, peer):
        copy = pltpu.make_async_remote_copy(
            src_ref=src, dst_ref=dst, send_sem=s, recv_sem=r, device_id=peer, device_id_type=MESH
        )
        return copy

    def wait_bytes(ref, sem):
        pltpu.make_async_copy(ref, ref, sem).wait()

    def their_state(i, carry):
        cols = lanes(other * NZ + i)
        xsend[i] = dot(k[:, cols], v[:, cols], 0, 0)
        return carry

    def my_state(i, carry):
        cols = lanes(c * NZ + i)
        own[i] = dot(k[:, cols], v[:, cols], 0, 0)
        return carry

    for n in range(2):
        loads[2 * n].wait()
        loads[2 * n + 1].wait()
        lax.fori_loop(4 * n, 4 * n + 4, their_state, 0, unroll=4)
    loads[4].wait()
    q8[0:4, :] = tq[0].astype(F32)
    q8[4:8, :] = tq[1].astype(F32)
    loads[5].wait()
    loads[6].wait()
    lax.fori_loop(0, 4, my_state, 0, unroll=4)
    pl.semaphore_wait(barrier, len(peers))
    for i in range(NZ):
        send(xsend.at[i], xrecv.at[i], x_s, x_r, partner).start()
    for d in (4, 3, 5, 2, 6, 1, 7, 0):
        for e in range(2):
            if d or e:
                core = other if e else c
                i = lax.rem(z + d, NZ)
                asking = q8.at[:, lanes(core * NZ + i)]
                send(asking, qrecv.at[z, c], q_s, q_r, {"sz": i, "sc": core}).start()
    qrecv[z, c] = q8[:, lanes(c * NZ + z)]
    loads[7].wait()
    loads[8].wait()
    lax.fori_loop(4, 8, my_state, 0, unroll=4)
    wait_bytes(xrecv, x_r)

    def chip_sum(i, dst):
        dst[...] = own[i] + xrecv[i]

    def span(j):
        return pl.ds(BOUNDS[j], BOUNDS[j + 1] - BOUNDS[j])

    for d in range(1, NZ):
        i = lax.rem(z + d, NZ)
        chip_sum(i, chip.at[i])
    for j in range(CHUNKS):
        for d in FAR_FIRST:
            i = lax.rem(z + d, NZ)
            send(chip.at[i, span(j)], recv1.at[z, span(j)], a_s, a_r.at[j], {"sz": i}).start()
    chip_sum(z, recv1.at[z])

    rows = lax.broadcasted_iota(jnp.int32, (256, 256), 0)
    columns = lax.broadcasted_iota(jnp.int32, (256, 256), 1)
    causal = columns <= rows

    def intra(h, carry):
        cols = lanes(h)
        top, bottom = q[0:256, cols], q[256:512, cols]
        s00 = jnp.where(causal, dot(top, k[0:256, cols], 1, 1), 0.0).astype(BF16)
        att[0:256, cols] = dot(s00, v[0:256, cols], 1, 0)
        s10 = dot(bottom, k[0:256, cols], 1, 1).astype(BF16)
        s11 = jnp.where(causal, dot(bottom, k[256:512, cols], 1, 1), 0.0).astype(BF16)
        att[256:512, cols] = dot(s10, v[0:256, cols], 1, 0) + dot(s11, v[256:512, cols], 1, 0)
        return carry

    def row_sum(j):
        part = slice(BOUNDS[j], BOUNDS[j + 1])
        wait_bytes(recv1.at[0 : NZ - 1, part], a_r.at[j])
        total = recv1[0, part, :]
        for n in range(1, NZ):
            total = total + recv1[n, part, :]
        rsend[part, :] = total
        yrecv[y, part, :] = total
        for d in (2, 1, 3):
            send(rsend.at[part], yrecv.at[y, part], y_s, y_r.at[j], away("sy", d)).start()

    def ready_steps():
        for copy in loads[10:]:
            copy.wait()
        k8[0:4, :] = tk[0].astype(F32)
        k8[4:8, :] = tk[1].astype(F32)
        v8[0:4, :] = tv[0].astype(F32)
        v8[4:8, :] = tv[1].astype(F32)
        k8s[...] = jnp.zeros_like(k8s)
        v8s[...] = jnp.zeros_like(v8s)
        k8s[4:8, :] = tk[0].astype(F32)
        v8s[4:8, :] = tv[0].astype(F32)
        row = lax.rem(lax.broadcasted_iota(jnp.int32, (8, D), 0), 4)
        column = lax.broadcasted_iota(jnp.int32, (8, D), 1)
        for n in range(4):
            live = (row == n) & (column < len_ref[n])
            mask[:, n * D : (n + 1) * D] = jnp.where(live, 1.0, 0.0)

    def suffix(h, carry):
        cols = lanes(h)
        query = q8[:, cols]
        scores = dot(query.astype(BF16), sk[:, cols], 1, 1) * mask[...]
        high = scores.astype(BF16).astype(F32)
        both = jnp.concatenate([high, scores - high], axis=0).astype(BF16)
        parts = dot(both, sv[:, cols], 1, 0)
        raw = parts[0:8] + parts[8:16]
        raw = raw + jnp.sum(query * k8[:, cols], axis=1, keepdims=True) * v8[:, cols]
        raw = raw + jnp.sum(query * k8s[:, cols], axis=1, keepdims=True) * v8s[:, cols]
        raw_out[:, cols] = raw
        return carry

    def priors(j):
        part = slice(BOUNDS[j], BOUNDS[j + 1])
        wait_bytes(yrecv.at[0 : NY - 1, part], y_r.at[j])
        before = jnp.zeros((BOUNDS[j + 1] - BOUNDS[j], D), F32)
        total = before
        for n in range(NY):
            before = before + jnp.where(n < y, yrecv[n, part, :], 0.0)
            total = total + yrecv[n, part, :]
        final[part, :] = total
        for n in range(NZ):
            send3[n, part, :] = before
            before = before + recv1[n, part, :]
        ship(j)
        recv3[z, part, :] = send3[z, part, :]

    def ship(j):
        for d in FAR_FIRST:
            i = lax.rem(z + d, NZ)
            send(send3.at[i, span(j)], recv3.at[z, span(j)], b_s, b_r.at[d], {"sz": i}).start()

    def answers():
        wait_bytes(q8.at[:, 0 : 15 * D], q_r)
        high = final[...].astype(BF16)
        low = (final[...] - high.astype(F32)).astype(BF16)
        asked = qrecv[...].reshape(NZ * 16, D).astype(BF16)
        told = dot(asked, high, 1, 0) + dot(asked, low, 1, 0)
        tell[...] = told.reshape(NZ, 2, 8, D)
        for d in (4, 3, 5, 2, 6, 1, 7, 0):
            for e in range(2):
                if d or e:
                    core = other if e else c
                    i = lax.rem(z + d, NZ)
                    slot = heard.at[c * NZ + z]
                    send(tell.at[i, core], slot, t_s, t_r, {"sz": i, "sc": core}).start()
        heard[c * NZ + z] = tell[z, c]

    loads[9].wait()
    work = {
        "intra": lambda a, b: lax.fori_loop(a, b, intra, 0, unroll=2),
        "suffix": lambda a, b: lax.fori_loop(a, b, suffix, 0, unroll=2),
        "steps": ready_steps,
        "sum": row_sum,
        "prior": priors,
        "answers": answers,
    }
    for name, *args in PLAN:
        work[name](*args)

    acc[...] = jnp.zeros_like(acc)

    def inter(h, prior):
        cols = lanes(h)
        low = prior.astype(BF16)
        for t in range(0, 512, 256):
            new = att[t : t + 256, cols] + dot(q[t : t + 256, cols], low, 1, 0)
            acc[t : t + 256, :] += new * new
            attb[t : t + 256, cols] = new.astype(BF16)

    for d in (0, *WAIT_ORDER):
        i = lax.rem(z + NZ - d, NZ)
        if d:
            wait_bytes(recv3.at[i], b_r.at[d])
        fwd[i] = recv3[i] + jnp.where(c == 0, own[i], 0.0)
        send(fwd.at[i], frecv.at[i], f_s, f_r, partner).start()

    def own_inter(i, carry):
        inter(c * NZ + i, recv3[i] + jnp.where(c == 1, xrecv[i], 0.0))
        return carry

    def their_inter(i, carry):
        inter(other * NZ + i, frecv[i])
        return carry

    lax.fori_loop(0, NZ, own_inter, 0, unroll=4)
    wait_bytes(heard.at[0:15], t_r)
    squares = jnp.zeros((8, D), F32)
    for h in range(16):
        cols = slice(h * D, (h + 1) * D)
        piece = raw_out[:, cols] + heard[h]
        raw_out[:, cols] = piece
        squares = squares + piece * piece
    msg[8:16, :] = jnp.broadcast_to(jnp.sum(squares, axis=1, keepdims=True), (8, D))
    raw_copy = pltpu.make_async_copy(raw_out, raw_hbm, out_sem.at[1])
    raw_copy.start()
    wait_bytes(frecv, f_r)
    lax.fori_loop(0, NZ, their_inter, 0, unroll=4)
    outs = [pltpu.make_async_copy(attb, att_out, out_sem.at[0])]
    outs[0].start()

    squares = lax.dot_general(
        jnp.ones((8, D), F32),
        acc[...],
        (((1,), (1,)), ((), ())),
        precision=lax.Precision.HIGHEST,
        preferred_element_type=F32,
    )
    for n in range(4):
        msg[n : n + 1, :] = squares[0:1, n * D : (n + 1) * D]
        msg[n + 4 : n + 5, :] = squares[0:1, n * D : (n + 1) * D]
    for d in (2, 1, 3):
        send(msg, sums_out.at[x], g_s, g_r, away("head", d)).start()
    outs.append(pltpu.make_async_copy(msg, sums_out.at[x], out_sem.at[2]))
    outs[1].start()
    outs.append(raw_copy)
    wait_bytes(xsend, x_s)
    wait_bytes(q8.at[:, 0 : 15 * D], q_s)
    wait_bytes(chip.at[0 : NZ - 1], a_s)
    wait_bytes(yrecv.at[0 : NY - 1], y_s)
    wait_bytes(send3.at[0 : NZ - 1], b_s)
    wait_bytes(fwd, f_s)
    wait_bytes(heard.at[0:15], t_s)
    wait_bytes(sums_out.at[0 : NX - 1], g_s)
    wait_bytes(sums_out.at[0 : NX - 1], g_r)
    for copy in outs:
        copy.wait()


def scale_kernel(att, sums, raw, gain, out, dec_out, held, dec, sem):
    copies = []
    for n in range(4):
        total = (sums[0, n : n + 1, :] + sums[1, n : n + 1, :]) + (
            sums[2, n : n + 1, :] + sums[3, n : n + 1, :]
        )
        scale = lax.rsqrt(jnp.broadcast_to(total, (D, D)).T / 8192.0 + 1e-06)
        for m in range(2):
            rows = slice(n * D + 64 * m, n * D + 64 * m + 64)
            part = scale[64 * m : 64 * m + 64]
            for h in range(16):
                cols = slice(h * D, (h + 1) * D)
                held[rows, cols] = (att[rows, cols].astype(F32) * part * gain[:, cols]).astype(BF16)
            copy = pltpu.make_async_copy(held.at[rows], out.at[rows], sem.at[2 * n + m])
            copy.start()
            copies.append(copy)
    steps = (sums[0, 8:16, 0:1] + sums[1, 8:16, 0:1]) + (sums[2, 8:16, 0:1] + sums[3, 8:16, 0:1])
    steps = lax.rsqrt(steps / 8192.0 + 1e-06)
    value = (raw[...] * steps * gain[...]).astype(BF16)
    dec[0] = value[0:4]
    dec[1] = value[4:8]
    copies.append(pltpu.make_async_copy(dec, dec_out, sem.at[8]))
    copies[8].start()
    for copy in copies:
        copy.wait()


def on_device(q, k, v, sk, sv, lengths, tq, tk, tv, gain):
    rows, width = q.shape
    sk = sk.reshape(-1, width)
    sv = sv.reshape(-1, width)
    anywhere = pl.BlockSpec(memory_space=pl.ANY)
    dma = pltpu.SemaphoreType.DMA
    steps = tq.shape

    def f32(*shape):
        return pltpu.VMEM(shape, F32)

    def bf16(*shape):
        return pltpu.VMEM(shape, BF16)

    att, sums, raw = pl.pallas_call(
        main_kernel,
        out_shape=(
            jax.ShapeDtypeStruct((rows, width), BF16),
            jax.ShapeDtypeStruct((NX, 16, D), F32),
            jax.ShapeDtypeStruct((8, width), F32),
        ),
        in_specs=[anywhere] * 9,
        out_specs=(anywhere, anywhere, anywhere),
        scratch_shapes=[
            pltpu.SMEM((4,), jnp.int32),
            f32(8, width),
            *[bf16(rows, width) for _ in range(5)],
            *[bf16(*steps) for _ in range(3)],
            *[f32(8, width) for _ in range(5)],
            f32(8, 512),
            f32(rows, width),
            bf16(rows, width),
            f32(rows, D),
            f32(NZ, D, D),
            f32(NZ, D, D),
            f32(NZ, D, D),
            f32(NZ, D, D),
            f32(NZ, D, D),
            f32(D, D),
            f32(NY, D, D),
            f32(NZ, D, D),
            f32(NZ, D, D),
            f32(NZ, 2, 8, D),
            f32(NZ, D, D),
            f32(NZ, D, D),
            f32(NZ, 2, 8, D),
            f32(2 * NZ, 8, D),
            f32(D, D),
            f32(16, D),
            dma((15,)),
            dma((3,)),
            *[dma(()) for _ in range(4)],
            dma(()),
            dma((CHUNKS,)),
            dma(()),
            dma((CHUNKS,)),
            dma(()),
            dma((NZ,)),
            *[dma(()) for _ in range(6)],
        ],
        compiler_params=pltpu.CompilerParams(
            collective_id=0, has_side_effects=True, vmem_limit_bytes=MAIN_VMEM
        ),
        name="main",
    )(*(pltpu.with_memory_space_constraint(a, pltpu.HBM) for a in (lengths, q, k, v, sk, sv, tq, tk, tv)))

    vmem = pl.BlockSpec(memory_space=pltpu.VMEM)
    return pl.pallas_call(
        scale_kernel,
        out_shape=(jax.ShapeDtypeStruct((rows, width), BF16), jax.ShapeDtypeStruct(steps, BF16)),
        in_specs=[vmem] * 4,
        out_specs=(anywhere, anywhere),
        scratch_shapes=[bf16(rows, width), bf16(*steps), dma((9,))],
        compiler_params=pltpu.CompilerParams(vmem_limit_bytes=12 << 20),
        name="scale",
    )(att, sums, raw, gain.reshape(1, width))


def solution(mesh):
    finer = Mesh(mesh.devices.reshape(NY, NZ, 2, NX), (*SEQ, "head"))
    return jax.shard_map(
        on_device,
        mesh=finer,
        in_specs=(
            P(SEQ, "head"),
            P(SEQ, "head"),
            P(SEQ, "head"),
            P(SEQ, None, "head"),
            P(SEQ, None, "head"),
            P(SEQ),
            P(None, SEQ, "head"),
            P(None, SEQ, "head"),
            P(None, SEQ, "head"),
            P("head"),
        ),
        out_specs=(P(SEQ, "head"), P(None, SEQ, "head")),
        check_vma=False,
    )
```

```python
import jax
import jax.numpy as jnp
from jax import lax
from jax.experimental import pallas as pl
from jax.experimental.pallas import tpu as pltpu
from jax.sharding import Mesh
from jax.sharding import PartitionSpec as P

D = 128
NY, NZ, NX = 4, 8, 4
AXES = {"sy": NY, "sz": NZ, "sc": 2, "head": NX}
SEQ = ("sy", "sz", "sc")
MESH = pl.DeviceIdType.MESH
F32 = jnp.float32
BF16 = jnp.bfloat16
BOUNDS = (0, 32, 64, 96, 128)
CHUNKS = len(BOUNDS) - 1
MAIN_VMEM = 36 << 20
FAR_FIRST = (4, 3, 5, 2, 6, 1, 7)
WAIT_ORDER = (1, 7, 2, 6, 3, 5, 4)
PLAN = (
    ("intra", 0, 12),
    ("sum", 0),
    ("intra", 12, 16),
    ("sum", 1),
    ("steps",),
    ("suffix", 0, 4),
    ("prior", 0),
    ("sum", 2),
    ("suffix", 4, 10),
    ("prior", 1),
    ("suffix", 10, 16),
    ("sum", 3),
    ("prior", 2),
    ("prior", 3),
    ("answers",),
)


def dot(a, b, ca, cb):
    return lax.dot_general(a, b, (((ca,), (cb,)), ((), ())), preferred_element_type=F32)


def away(axis, step):
    size = AXES[axis]
    return {axis: lax.rem(lax.axis_index(axis) + step, size)}


def lanes(head):
    return pl.ds(pl.multiple_of(head * D, D), D)


def main_kernel(
    len_hbm, q_hbm, k_hbm, v_hbm, sk_hbm, sv_hbm, tq_hbm, tk_hbm, tv_hbm,
    att_out, sums_out, raw_hbm,
    len_ref, raw_out,
    q, k, v, sk, sv, tq, tk, tv, q8, k8, v8, k8s, v8s, mask,
    att, attb, acc, own, xsend, xrecv, chip, recv1, rsend, yrecv, send3, recv3,
    qrecv, fwd, frecv, tell, heard, final, msg,
    ld, out_sem, x_s, x_r, q_s, q_r, a_s, a_r, y_s, y_r, b_s, b_r, f_s, f_r, t_s, t_r, g_s, g_r,
):
    y, z, c, x = (lax.axis_index(a) for a in ("sy", "sz", "sc", "head"))
    other = 1 - c
    partner = {"sc": other}
    barrier = pltpu.get_barrier_semaphore()
    peers = [partner]
    peers += [away("sz", d) for d in range(1, NZ)]
    peers += [away("sz", d) | partner for d in range(1, NZ)]
    peers += [away("sy", d) for d in range(1, NY)]
    peers += [away("head", d) for d in range(1, NX)]
    for peer in peers:
        pl.semaphore_signal(barrier, inc=1, device_id=peer, device_id_type=MESH)

    quarter = NZ * D // 2

    def part_of(core, n):
        return pl.ds(pl.multiple_of((2 * core + n) * quarter, quarter), quarter)

    loads = []
    for core in (other, c):
        for n in range(2):
            cols = part_of(core, n)
            loads.append((k_hbm.at[:, cols], k.at[:, cols]))
            loads.append((v_hbm.at[:, cols], v.at[:, cols]))
        if core is other:
            loads.append((tq_hbm, tq))
    loads += [(q_hbm, q), (len_hbm, len_ref), (tk_hbm, tk), (tv_hbm, tv), (sk_hbm, sk), (sv_hbm, sv)]
    loads = [pltpu.make_async_copy(src, dst, ld.at[n]) for n, (src, dst) in enumerate(loads)]
    for copy in loads[:9]:
        copy.start()

    def send(src, dst, s, r, peer):
        copy = pltpu.make_async_remote_copy(
            src_ref=src, dst_ref=dst, send_sem=s, recv_sem=r, device_id=peer, device_id_type=MESH
        )
        return copy

    def wait_bytes(ref, sem):
        pltpu.make_async_copy(ref, ref, sem).wait()

    def their_state(i, carry):
        cols = lanes(other * NZ + i)
        xsend[i] = dot(k[:, cols], v[:, cols], 0, 0)
        return carry

    def my_state(i, carry):
        cols = lanes(c * NZ + i)
        own[i] = dot(k[:, cols], v[:, cols], 0, 0)
        return carry

    for n in range(2):
        loads[2 * n].wait()
        loads[2 * n + 1].wait()
        lax.fori_loop(4 * n, 4 * n + 4, their_state, 0, unroll=4)
    loads[4].wait()
    q8[0:4, :] = tq[0].astype(F32)
    q8[4:8, :] = tq[1].astype(F32)
    loads[5].wait()
    loads[6].wait()
    lax.fori_loop(0, 4, my_state, 0, unroll=4)
    for copy in loads[9:]:
        copy.start()
    pl.semaphore_wait(barrier, len(peers))
    for i in range(NZ):
        send(xsend.at[i], xrecv.at[i], x_s, x_r, partner).start()
    for d in (4, 3, 5, 2, 6, 1, 7, 0):
        for e in range(2):
            if d or e:
                core = other if e else c
                i = lax.rem(z + d, NZ)
                asking = q8.at[:, lanes(core * NZ + i)]
                send(asking, qrecv.at[z, c], q_s, q_r, {"sz": i, "sc": core}).start()
    qrecv[z, c] = q8[:, lanes(c * NZ + z)]
    loads[7].wait()
    loads[8].wait()
    lax.fori_loop(4, 8, my_state, 0, unroll=4)
    wait_bytes(xrecv, x_r)

    def chip_sum(i, dst):
        dst[...] = own[i] + xrecv[i]

    def span(j):
        return pl.ds(BOUNDS[j], BOUNDS[j + 1] - BOUNDS[j])

    for d in range(1, NZ):
        i = lax.rem(z + d, NZ)
        chip_sum(i, chip.at[i])
    for j in range(CHUNKS):
        for d in FAR_FIRST:
            i = lax.rem(z + d, NZ)
            send(chip.at[i, span(j)], recv1.at[z, span(j)], a_s, a_r.at[j], {"sz": i}).start()
    chip_sum(z, recv1.at[z])

    rows = lax.broadcasted_iota(jnp.int32, (256, 256), 0)
    columns = lax.broadcasted_iota(jnp.int32, (256, 256), 1)
    causal = columns <= rows

    def intra(h, carry):
        cols = lanes(h)
        top, bottom = q[0:256, cols], q[256:512, cols]
        s00 = jnp.where(causal, dot(top, k[0:256, cols], 1, 1), 0.0).astype(BF16)
        att[0:256, cols] = dot(s00, v[0:256, cols], 1, 0)
        s10 = dot(bottom, k[0:256, cols], 1, 1).astype(BF16)
        s11 = jnp.where(causal, dot(bottom, k[256:512, cols], 1, 1), 0.0).astype(BF16)
        att[256:512, cols] = dot(s10, v[0:256, cols], 1, 0) + dot(s11, v[256:512, cols], 1, 0)
        return carry

    def row_sum(j):
        part = slice(BOUNDS[j], BOUNDS[j + 1])
        wait_bytes(recv1.at[0 : NZ - 1, part], a_r.at[j])
        total = recv1[0, part, :]
        for n in range(1, NZ):
            total = total + recv1[n, part, :]
        rsend[part, :] = total
        yrecv[y, part, :] = total
        for d in (2, 1, 3):
            send(rsend.at[part], yrecv.at[y, part], y_s, y_r.at[j], away("sy", d)).start()

    def ready_steps():
        for copy in loads[10:]:
            copy.wait()
        k8[0:4, :] = tk[0].astype(F32)
        k8[4:8, :] = tk[1].astype(F32)
        v8[0:4, :] = tv[0].astype(F32)
        v8[4:8, :] = tv[1].astype(F32)
        k8s[...] = jnp.zeros_like(k8s)
        v8s[...] = jnp.zeros_like(v8s)
        k8s[4:8, :] = tk[0].astype(F32)
        v8s[4:8, :] = tv[0].astype(F32)
        row = lax.rem(lax.broadcasted_iota(jnp.int32, (8, D), 0), 4)
        column = lax.broadcasted_iota(jnp.int32, (8, D), 1)
        for n in range(4):
            live = (row == n) & (column < len_ref[n])
            mask[:, n * D : (n + 1) * D] = jnp.where(live, 1.0, 0.0)

    def suffix(h, carry):
        cols = lanes(h)
        query = q8[:, cols]
        scores = dot(query.astype(BF16), sk[:, cols], 1, 1) * mask[...]
        high = scores.astype(BF16).astype(F32)
        both = jnp.concatenate([high, scores - high], axis=0).astype(BF16)
        parts = dot(both, sv[:, cols], 1, 0)
        raw = parts[0:8] + parts[8:16]
        raw = raw + jnp.sum(query * k8[:, cols], axis=1, keepdims=True) * v8[:, cols]
        raw = raw + jnp.sum(query * k8s[:, cols], axis=1, keepdims=True) * v8s[:, cols]
        raw_out[:, cols] = raw
        return carry

    def priors(j):
        part = slice(BOUNDS[j], BOUNDS[j + 1])
        wait_bytes(yrecv.at[0 : NY - 1, part], y_r.at[j])
        before = jnp.zeros((BOUNDS[j + 1] - BOUNDS[j], D), F32)
        total = before
        for n in range(NY):
            before = before + jnp.where(n < y, yrecv[n, part, :], 0.0)
            total = total + yrecv[n, part, :]
        final[part, :] = total
        for n in range(NZ):
            send3[n, part, :] = before
            before = before + recv1[n, part, :]
        ship(j)
        recv3[z, part, :] = send3[z, part, :]

    def ship(j):
        for d in FAR_FIRST:
            i = lax.rem(z + d, NZ)
            send(send3.at[i, span(j)], recv3.at[z, span(j)], b_s, b_r.at[d], {"sz": i}).start()

    def answers():
        wait_bytes(q8.at[:, 0 : 15 * D], q_r)
        high = final[...].astype(BF16)
        low = (final[...] - high.astype(F32)).astype(BF16)
        asked = qrecv[...].reshape(NZ * 16, D).astype(BF16)
        told = dot(asked, high, 1, 0) + dot(asked, low, 1, 0)
        tell[...] = told.reshape(NZ, 2, 8, D)
        for d in (4, 3, 5, 2, 6, 1, 7, 0):
            for e in range(2):
                if d or e:
                    core = other if e else c
                    i = lax.rem(z + d, NZ)
                    slot = heard.at[c * NZ + z]
                    send(tell.at[i, core], slot, t_s, t_r, {"sz": i, "sc": core}).start()
        heard[c * NZ + z] = tell[z, c]

    loads[9].wait()
    work = {
        "intra": lambda a, b: lax.fori_loop(a, b, intra, 0, unroll=2),
        "suffix": lambda a, b: lax.fori_loop(a, b, suffix, 0, unroll=2),
        "steps": ready_steps,
        "sum": row_sum,
        "prior": priors,
        "answers": answers,
    }
    for name, *args in PLAN:
        work[name](*args)

    acc[...] = jnp.zeros_like(acc)

    def inter(h, prior):
        cols = lanes(h)
        low = prior.astype(BF16)
        for t in range(0, 512, 256):
            new = att[t : t + 256, cols] + dot(q[t : t + 256, cols], low, 1, 0)
            acc[t : t + 256, :] += new * new
            attb[t : t + 256, cols] = new.astype(BF16)

    for d in (0, *WAIT_ORDER):
        i = lax.rem(z + NZ - d, NZ)
        if d:
            wait_bytes(recv3.at[i], b_r.at[d])
        fwd[i] = recv3[i] + jnp.where(c == 0, own[i], 0.0)
        send(fwd.at[i], frecv.at[i], f_s, f_r, partner).start()

    def own_inter(i, carry):
        inter(c * NZ + i, recv3[i] + jnp.where(c == 1, xrecv[i], 0.0))
        return carry

    def their_inter(i, carry):
        inter(other * NZ + i, frecv[i])
        return carry

    lax.fori_loop(0, NZ, own_inter, 0, unroll=4)
    wait_bytes(heard.at[0:15], t_r)
    squares = jnp.zeros((8, D), F32)
    for h in range(16):
        cols = slice(h * D, (h + 1) * D)
        piece = raw_out[:, cols] + heard[h]
        raw_out[:, cols] = piece
        squares = squares + piece * piece
    msg[8:16, :] = jnp.broadcast_to(jnp.sum(squares, axis=1, keepdims=True), (8, D))
    raw_copy = pltpu.make_async_copy(raw_out, raw_hbm, out_sem.at[1])
    raw_copy.start()
    wait_bytes(frecv, f_r)
    lax.fori_loop(0, NZ, their_inter, 0, unroll=4)
    outs = [pltpu.make_async_copy(attb, att_out, out_sem.at[0])]
    outs[0].start()

    squares = lax.dot_general(
        jnp.ones((8, D), F32),
        acc[...],
        (((1,), (1,)), ((), ())),
        precision=lax.Precision.HIGHEST,
        preferred_element_type=F32,
    )
    for n in range(4):
        msg[n : n + 1, :] = squares[0:1, n * D : (n + 1) * D]
        msg[n + 4 : n + 5, :] = squares[0:1, n * D : (n + 1) * D]
    for d in (2, 1, 3):
        send(msg, sums_out.at[x], g_s, g_r, away("head", d)).start()
    outs.append(pltpu.make_async_copy(msg, sums_out.at[x], out_sem.at[2]))
    outs[1].start()
    outs.append(raw_copy)
    wait_bytes(xsend, x_s)
    wait_bytes(q8.at[:, 0 : 15 * D], q_s)
    wait_bytes(chip.at[0 : NZ - 1], a_s)
    wait_bytes(yrecv.at[0 : NY - 1], y_s)
    wait_bytes(send3.at[0 : NZ - 1], b_s)
    wait_bytes(fwd, f_s)
    wait_bytes(heard.at[0:15], t_s)
    wait_bytes(sums_out.at[0 : NX - 1], g_s)
    wait_bytes(sums_out.at[0 : NX - 1], g_r)
    for copy in outs:
        copy.wait()


def scale_kernel(att, sums, raw, gain, out, dec_out, held, dec, sem):
    copies = []
    for n in range(4):
        total = (sums[0, n : n + 1, :] + sums[1, n : n + 1, :]) + (
            sums[2, n : n + 1, :] + sums[3, n : n + 1, :]
        )
        scale = lax.rsqrt(jnp.broadcast_to(total, (D, D)).T / 8192.0 + 1e-06)
        for m in range(2):
            rows = slice(n * D + 64 * m, n * D + 64 * m + 64)
            part = scale[64 * m : 64 * m + 64]
            for h in range(16):
                cols = slice(h * D, (h + 1) * D)
                held[rows, cols] = (att[rows, cols].astype(F32) * part * gain[:, cols]).astype(BF16)
            copy = pltpu.make_async_copy(held.at[rows], out.at[rows], sem.at[2 * n + m])
            copy.start()
            copies.append(copy)
    steps = (sums[0, 8:16, 0:1] + sums[1, 8:16, 0:1]) + (sums[2, 8:16, 0:1] + sums[3, 8:16, 0:1])
    steps = lax.rsqrt(steps / 8192.0 + 1e-06)
    value = (raw[...] * steps * gain[...]).astype(BF16)
    dec[0] = value[0:4]
    dec[1] = value[4:8]
    copies.append(pltpu.make_async_copy(dec, dec_out, sem.at[8]))
    copies[8].start()
    for copy in copies:
        copy.wait()


def on_device(q, k, v, sk, sv, lengths, tq, tk, tv, gain):
    rows, width = q.shape
    sk = sk.reshape(-1, width)
    sv = sv.reshape(-1, width)
    anywhere = pl.BlockSpec(memory_space=pl.ANY)
    dma = pltpu.SemaphoreType.DMA
    steps = tq.shape

    def f32(*shape):
        return pltpu.VMEM(shape, F32)

    def bf16(*shape):
        return pltpu.VMEM(shape, BF16)

    att, sums, raw = pl.pallas_call(
        main_kernel,
        out_shape=(
            jax.ShapeDtypeStruct((rows, width), BF16),
            jax.ShapeDtypeStruct((NX, 16, D), F32),
            jax.ShapeDtypeStruct((8, width), F32),
        ),
        in_specs=[anywhere] * 9,
        out_specs=(anywhere, anywhere, anywhere),
        scratch_shapes=[
            pltpu.SMEM((4,), jnp.int32),
            f32(8, width),
            *[bf16(rows, width) for _ in range(5)],
            *[bf16(*steps) for _ in range(3)],
            *[f32(8, width) for _ in range(5)],
            f32(8, 512),
            f32(rows, width),
            bf16(rows, width),
            f32(rows, D),
            f32(NZ, D, D),
            f32(NZ, D, D),
            f32(NZ, D, D),
            f32(NZ, D, D),
            f32(NZ, D, D),
            f32(D, D),
            f32(NY, D, D),
            f32(NZ, D, D),
            f32(NZ, D, D),
            f32(NZ, 2, 8, D),
            f32(NZ, D, D),
            f32(NZ, D, D),
            f32(NZ, 2, 8, D),
            f32(2 * NZ, 8, D),
            f32(D, D),
            f32(16, D),
            dma((15,)),
            dma((3,)),
            *[dma(()) for _ in range(4)],
            dma(()),
            dma((CHUNKS,)),
            dma(()),
            dma((CHUNKS,)),
            dma(()),
            dma((NZ,)),
            *[dma(()) for _ in range(6)],
        ],
        compiler_params=pltpu.CompilerParams(
            collective_id=0, has_side_effects=True, vmem_limit_bytes=MAIN_VMEM
        ),
        name="main",
    )(*(pltpu.with_memory_space_constraint(a, pltpu.HBM) for a in (lengths, q, k, v, sk, sv, tq, tk, tv)))

    vmem = pl.BlockSpec(memory_space=pltpu.VMEM)
    return pl.pallas_call(
        scale_kernel,
        out_shape=(jax.ShapeDtypeStruct((rows, width), BF16), jax.ShapeDtypeStruct(steps, BF16)),
        in_specs=[vmem] * 4,
        out_specs=(anywhere, anywhere),
        scratch_shapes=[bf16(rows, width), bf16(*steps), dma((9,))],
        compiler_params=pltpu.CompilerParams(vmem_limit_bytes=12 << 20),
        name="scale",
    )(att, sums, raw, gain.reshape(1, width))


def solution(mesh):
    finer = Mesh(mesh.devices.reshape(NY, NZ, 2, NX), (*SEQ, "head"))
    return jax.shard_map(
        on_device,
        mesh=finer,
        in_specs=(
            P(SEQ, "head"),
            P(SEQ, "head"),
            P(SEQ, "head"),
            P(SEQ, None, "head"),
            P(SEQ, None, "head"),
            P(SEQ),
            P(None, SEQ, "head"),
            P(None, SEQ, "head"),
            P(None, SEQ, "head"),
            P("head"),
        ),
        out_specs=(P(SEQ, "head"), P(None, SEQ, "head")),
        check_vma=False,
    )
```
